32 devices in a mesh: depth: 2 (over y), row: 4 (over z), col: 4 (over x, core).
Axes of the slice: x: 2, y: 2, z: 4, core: 2. Of those that a mesh axis runs over, the one named last changes fastest.
Arguments:
- prop: bfloat16 [2, 2, 8192, 8192], P('depth', None, 'row', 'col'), may hold values from -0.046875 to 0.046875
- source: float32 [8192, 256], P(('row', 'col')), may hold values from -6 to 6
- down_init: float32 [2, 8192, 256], P('depth', ('row', 'col')), may hold values from -6 to 6
- up_init: float32 [2, 8192, 256], P('depth', ('row', 'col')), may hold values from -6 to 6
- refl_down: float32 [2, 8192], P('depth', ('row', 'col')), may hold values from -0.6 to 0.6
- refl_up: float32 [2, 8192], P('depth', ('row', 'col')), may hold values from -0.6 to 0.6
Outputs:
- down_field: float32 [2, 8192, 256], P('depth', ('row', 'col'))
- up_field: float32 [2, 8192, 256], P('depth', ('row', 'col'))
The draws below stay inside these ranges and needn't reach their ends.
All inputs are finite; a program needn't handle non-finite values.
Results may differ from the reference program's by a relative error of at most 0.0041.
Values may be sent and summed in bfloat16 or wider, within the bound.
No kernel may reach another device: no remote copies, remote signals or barrier semaphores. Data moves between devices by JAX's collectives and lax.ppermute only.
A program may use at most 64 MiB of HBM per device.

```python
import jax
import jax.numpy as jnp
from jax import lax

N = 8192
SRC = 128
PASSES = 2
LEVELS = 2
STRIP = 512
N_ROW = 4
N_COL = 4


def block_scale(own_key, dims, shards, least, top_value):
    def one(axis_at, blocks):
        heights = jax.random.uniform(jax.random.fold_in(jax.random.fold_in(own_key, 6), axis_at), (blocks,), jnp.float32, least / len(shards), top_value / len(shards))
        return jnp.repeat(jnp.exp(heights), dims[axis_at] // blocks).reshape((-1,) + (1,) * (len(dims) - axis_at - 1))

    factor_of = one(*shards[0])
    for cut in shards[1:]:
        factor_of = factor_of * one(*cut)
    return factor_of


def gaussian(own_key, shape, spread, reach, pieces=(), held_as=jnp.bfloat16):
    array = spread * jax.random.normal(own_key, shape, jnp.float32)
    if pieces:
        array = array * block_scale(own_key, shape, pieces, -0.22, 0.18)
    return jnp.clip(array, -reach, reach).astype(held_as)


def setup_inputs(seed: int = 0) -> dict:
    keys = jax.random.split(jax.random.key(seed), 7)
    prop = gaussian(keys[0], (LEVELS, 2, N, N), (2 * N) ** -0.5, 0.046875, ((0, 2), (2, 4), (3, 4)))
    source = gaussian(keys[1], (N, 2 * SRC), 1.0, 6.0, ((0, 16),), jnp.float32)
    down_init = gaussian(keys[2], (LEVELS, N, 2 * SRC), 1.0, 6.0, ((0, 2), (1, 16)), jnp.float32)
    up_init = gaussian(keys[3], (LEVELS, N, 2 * SRC), 1.0, 6.0, ((0, 2), (1, 16)), jnp.float32)
    refl_down = jnp.clip(jax.random.uniform(keys[4], (LEVELS, N), jnp.float32, -0.6, 0.6) * block_scale(keys[4], (LEVELS, N), ((0, 2), (1, 16)), -0.4, 0.0), -0.6, 0.6)
    refl_up = jnp.clip(jax.random.uniform(keys[5], (LEVELS, N), jnp.float32, -0.6, 0.6) * block_scale(keys[5], (LEVELS, N), ((0, 2), (1, 16)), -0.4, 0.0), -0.6, 0.6)
    return dict(prop=prop, source=source, down_init=down_init, up_init=up_init, refl_down=refl_down, refl_up=refl_up)


def to_columns(field):
    return field.reshape(N_ROW, N_COL, STRIP, 2 * SRC).transpose(1, 0, 2, 3).reshape(N, 2 * SRC)


def to_grid(field):
    return field.reshape(N_COL, N_ROW, STRIP, 2 * SRC).transpose(1, 0, 2, 3).reshape(N, 2 * SRC)


def complex_join(first, second):
    real_part = first[:, :SRC] - second[:, SRC:]
    imag_part = first[:, SRC:] + second[:, :SRC]
    return jnp.concatenate([real_part, imag_part], axis=1)


def level_products(inputs):
    weights, down_low, up_low = inputs
    columns = to_columns(down_low)
    trans = complex_join(jnp.dot(weights[0], columns, preferred_element_type=jnp.float32),
                         jnp.dot(weights[1], columns, preferred_element_type=jnp.float32))
    block_rows = N // N_ROW

    def add_block(total, index):
        start = (index * block_rows).astype(jnp.int32)
        weight_real = lax.dynamic_slice_in_dim(weights[0], start, block_rows, 0)
        weight_imag = lax.dynamic_slice_in_dim(weights[1], start, block_rows, 0)
        block = lax.dynamic_slice_in_dim(up_low, start, block_rows, 0)
        partial_value = complex_join(jnp.dot(weight_real.T, block, preferred_element_type=jnp.float32),
                               jnp.dot(weight_imag.T, block, preferred_element_type=jnp.float32))
        return total + partial_value, None

    back_columns, _ = lax.scan(add_block, jnp.zeros((N, 2 * SRC), jnp.float32),
                               jnp.arange(N_ROW, dtype=jnp.int32))
    return trans, to_grid(back_columns)


def reference(prop, source, down_init, up_init, refl_down, refl_up):
    down = down_init
    up = up_init
    for sweep in range(PASSES):
        trans, back = lax.map(level_products, (prop, down.astype(jnp.bfloat16), up.astype(jnp.bfloat16)))
        above = jnp.concatenate([source[None], trans[:-1]], axis=0)
        below = jnp.concatenate([back[1:], jnp.zeros_like(back[:1])], axis=0)
        down = above + refl_down[:, :, None] * back
        up = below + refl_up[:, :, None] * trans
    return down, up
```

```python
import functools

import jax
import jax.numpy as jnp
from jax import lax
from jax.experimental import pallas as pl
from jax.experimental.pallas import tpu as pltpu
from jax.sharding import PartitionSpec as P

PASSES = 2
F32 = jnp.float32
BF16 = jnp.bfloat16
WHOLE = pl.BlockSpec(memory_space=pltpu.VMEM)
CONTRACT_ROWS = (((0,), (0,)), ((), ()))


def ring_device(place, size):
    half = (size + 1) // 2
    if isinstance(place, int):
        return 2 * place if place < half else 2 * (size - 1 - place) + 1
    return jnp.where(place < half, 2 * place, 2 * (size - 1 - place) + 1)


def ring_place(device, size):
    return jnp.where(lax.rem(device, 2) == 0, device // 2, size - 1 - device // 2)


def ring_block(behind, size):
    place = ring_place(lax.axis_index("row"), size)
    return ring_device(lax.rem(place - behind + size, size), size)


def ring_hop(x, size):
    pairs = [(ring_device(p, size), ring_device((p + 1) % size, size)) for p in range(size)]
    return lax.ppermute(x, "row", pairs)


def col_swap(x, bit):
    return lax.ppermute(x, "col", [(c, c ^ bit) for c in range(lax.axis_size("col"))])


def depth_shift(x, by):
    peers = lax.axis_size("depth")
    return lax.ppermute(x, "depth", [(i, i + by) for i in range(peers) if 0 <= i + by < peers])


def call(kernel, outs, name, flops, *args):
    moved = sum(a.size * a.dtype.itemsize for a in args)
    return pl.pallas_call(
        kernel,
        in_specs=[WHOLE] * len(args),
        out_specs=[WHOLE] * len(outs),
        out_shape=outs,
        name=name,
        cost_estimate=pl.CostEstimate(flops=flops, bytes_accessed=moved // 8, transcendentals=0),
        compiler_params=pltpu.CompilerParams(vmem_limit_bytes=12 * 2**20),
    )(*args)


def rows_at(block, strip):
    return pl.ds(pl.multiple_of(block * strip, strip), strip)


def place_block(pair_ref, block_ref, rows, sources):
    values = block_ref[...]
    pair_ref[0, rows, :] = values
    pair_ref[1, rows, :sources] = -values[:, sources:]
    pair_ref[1, rows, sources:] = values[:, :sources]


def down_first(size, strip, sources, w_ref, *refs):
    blocks, pair_ref, out_ref = refs[:size], refs[size], refs[size + 1]
    for s in range(size):
        place_block(pair_ref, blocks[s], rows_at(ring_block(s, size), strip), sources)
    me = lax.axis_index("col")
    for k in range(2):
        down_dot(w_ref, pair_ref, rows_at(me ^ (1 + 2 * k), strip), out_ref, k)


def down_dot(w_ref, pair_ref, rows, out_ref, k):
    out_ref[k] = jnp.dot(w_ref[0, 0, rows, :], pair_ref[0], preferred_element_type=F32) + jnp.dot(
        w_ref[0, 1, rows, :], pair_ref[1], preferred_element_type=F32
    )


def down_second(strip, w_ref, pair_ref, out_ref):
    me = lax.axis_index("col")
    for k in range(2):
        down_dot(w_ref, pair_ref, rows_at(me ^ (2 * k), strip), out_ref, k)


def up_dot(w_ref, pair_ref, columns):
    return lax.dot_general(
        w_ref[0, 0, :, columns], pair_ref[0], CONTRACT_ROWS, preferred_element_type=F32
    ) + lax.dot_general(w_ref[0, 1, :, columns], pair_ref[1], CONTRACT_ROWS, preferred_element_type=F32)


def up_first(size, strip, sources, w_ref, *refs):
    blocks, pair_ref, out_ref = refs[:4], refs[4], refs[5]
    me = lax.axis_index("col")
    for s in range(4):
        place_block(pair_ref, blocks[s], rows_at(me ^ s, strip), sources)
    out_ref[...] = up_dot(w_ref, pair_ref, rows_at(ring_block(1, size), strip)).astype(BF16)


def up_rest(size, strip, w_ref, pair_ref, *out_refs):
    for s in range(2, size + 1):
        out_refs[s - 2][...] = up_dot(w_ref, pair_ref, rows_at(ring_block(s % size, size), strip))


def body(prop, source, down_init, up_init, refl_down, refl_up):
    size = lax.axis_size("row")
    assert lax.axis_size("col") == 4
    strip = down_init.shape[1]
    width = down_init.shape[2]
    sources = width // 2
    tall, wide = prop.shape[2], prop.shape[3]
    shape = functools.partial(jax.ShapeDtypeStruct)
    dot_flops = 4 * strip * width
    at_surface = lax.axis_index("depth") == 0
    refl_above = refl_down[0][:, None]
    refl_below = refl_up[0][:, None]
    down_low = down_init[0].astype(BF16)
    up_low = up_init[0].astype(BF16)
    for sweep in range(PASSES):
        far = col_swap(up_low, 2)
        blocks_up = [up_low, col_swap(up_low, 1), far, col_swap(far, 1)]
        blocks_down = [down_low]
        for s in range(size - 1):
            blocks_down.append(ring_hop(blocks_down[-1], size))
        pair_up, travelling = call(
            functools.partial(up_first, size, strip, sources),
            [shape((2, tall, width), BF16), shape((strip, width), BF16)],
            "up_first", dot_flops * tall, prop, *blocks_up,
        )
        own_up = call(
            functools.partial(up_rest, size, strip),
            [shape((strip, width), F32)] * (size - 1),
            "up_rest", dot_flops * tall * (size - 1), prop, pair_up,
        )
        for s in range(size - 2):
            travelling = (ring_hop(travelling, size).astype(F32) + own_up[s]).astype(BF16)
        back = ring_hop(travelling, size).astype(F32) + own_up[size - 2]
        from_below = depth_shift(back.astype(BF16), -1).astype(F32)
        pair_down, to_sibling = call(
            functools.partial(down_first, size, strip, sources),
            [shape((2, wide, width), BF16), shape((2, strip, width), F32)],
            "down_first", dot_flops * wide * 2, prop, *blocks_down,
        )
        (own_down,) = call(
            functools.partial(down_second, strip),
            [shape((2, strip, width), F32)],
            "down_second", dot_flops * wide * 2, prop, pair_down,
        )
        both = own_down + col_swap(to_sibling, 1)
        trans = both[0] + col_swap(both[1].astype(BF16), 2).astype(F32)
        from_above = depth_shift(trans.astype(BF16), 1).astype(F32)
        down = jnp.where(at_surface, source, from_above) + refl_above * back
        up = from_below + refl_below * trans
        down_low = down.astype(BF16)
        up_low = up.astype(BF16)
    return (down[None], up[None])


def solution(mesh):
    placed = (
        P("depth", None, "row", "col"),
        P(("row", "col"), None),
        P("depth", ("row", "col"), None),
        P("depth", ("row", "col"), None),
        P("depth", ("row", "col")),
        P("depth", ("row", "col")),
    )
    return jax.shard_map(
        body,
        mesh=mesh,
        in_specs=placed,
        out_specs=(P("depth", ("row", "col"), None), P("depth", ("row", "col"), None)),
        check_vma=False,
    )
```

```python
import functools

import jax
import jax.numpy as jnp
from jax import lax
from jax.experimental import pallas as pl
from jax.experimental.pallas import tpu as pltpu
from jax.sharding import PartitionSpec as P

PASSES = 2
F32 = jnp.float32
BF16 = jnp.bfloat16
WHOLE = pl.BlockSpec(memory_space=pltpu.VMEM)
UNREAD = pl.BlockSpec(memory_space=pl.ANY)
LANES = 128
DECLARED = 21 * 10**9
CONTRACT_ROWS = (((0,), (0,)), ((), ()))


def ring_device(place, size):
    half = (size + 1) // 2
    if isinstance(place, int):
        return 2 * place if place < half else 2 * (size - 1 - place) + 1
    return jnp.where(place < half, 2 * place, 2 * (size - 1 - place) + 1)


def ring_place(device, size):
    return jnp.where(lax.rem(device, 2) == 0, device // 2, size - 1 - device // 2)


def ring_block(behind, size):
    place = ring_place(lax.axis_index("row"), size)
    return ring_device(lax.rem(place - behind + size, size), size)


def ring_hop(x, size):
    pairs = [(ring_device(p, size), ring_device((p + 1) % size, size)) for p in range(size)]
    return lax.ppermute(x, "row", pairs)


def col_swap(x, bit):
    return lax.ppermute(x, "col", [(c, c ^ bit) for c in range(lax.axis_size("col"))])


def depth_shift(x, by):
    peers = lax.axis_size("depth")
    return lax.ppermute(x, "depth", [(i, i + by) for i in range(peers) if 0 <= i + by < peers])


def call(kernel, outs, name, args, after=()):
    count = len(args)

    def ordered(*refs):
        kernel(*refs[:count], *refs[count + len(after) :])

    return pl.pallas_call(
        ordered,
        in_specs=[WHOLE] * count + [UNREAD] * len(after),
        out_specs=[WHOLE] * len(outs),
        out_shape=outs,
        name=name,
        cost_estimate=pl.CostEstimate(flops=DECLARED, bytes_accessed=2**20, transcendentals=0),
        compiler_params=pltpu.CompilerParams(vmem_limit_bytes=12 * 2**20),
    )(*args, *after)


def array(shape, dtype):
    return jax.ShapeDtypeStruct(shape, dtype)


def behind(x, *others):
    return lax.optimization_barrier((x, *others))[0]


def rows_at(block, strip):
    return pl.ds(pl.multiple_of(block * strip, strip), strip)


def hold(prop, after):
    def kernel(w_ref, _, out_ref, sem):
        copy = pltpu.make_async_copy(w_ref, out_ref, sem)
        copy.start()
        copy.wait()

    return pl.pallas_call(
        kernel,
        in_specs=[pl.BlockSpec(memory_space=pltpu.HBM), UNREAD],
        out_specs=WHOLE,
        out_shape=pltpu.VMEM(prop.shape, prop.dtype),
        scratch_shapes=[pltpu.SemaphoreType.DMA],
        name="hold",
        cost_estimate=pl.CostEstimate(flops=0, bytes_accessed=40 * prop.size, transcendentals=0),
        compiler_params=pltpu.CompilerParams(vmem_limit_bytes=36 * 2**20),
    )(prop, after)


def place_block(pair_ref, block_ref, rows, sources):
    values = block_ref[...]
    pair_ref[0, rows, :] = values
    pair_ref[1, rows, :sources] = -values[:, sources:]
    pair_ref[1, rows, sources:] = values[:, :sources]


def spread(refl_ref):
    return jnp.broadcast_to(refl_ref[...], (LANES, refl_ref.shape[1])).T


def scaled(refl_ref, values):
    factor = refl_ref[...]
    pieces = [factor * values[:, k : k + LANES] for k in range(0, values.shape[1], LANES)]
    return jnp.concatenate(pieces, axis=1)


def ready_kernel(field_ref, refl_ref, low_ref, factor_ref):
    low_ref[...] = field_ref[0].astype(BF16)
    factor_ref[...] = spread(refl_ref)


def down_dot(w_ref, pair_ref, rows):
    return jnp.dot(w_ref[0, 0, rows, :], pair_ref[0], preferred_element_type=F32) + jnp.dot(
        w_ref[0, 1, rows, :], pair_ref[1], preferred_element_type=F32
    )


def up_dot(w_ref, pair_ref, columns):
    return lax.dot_general(
        w_ref[0, 0, :, columns], pair_ref[0], CONTRACT_ROWS, preferred_element_type=F32
    ) + lax.dot_general(w_ref[0, 1, :, columns], pair_ref[1], CONTRACT_ROWS, preferred_element_type=F32)


def down_sibling_kernel(size, strip, sources, w_ref, *refs):
    blocks, pair_ref, out_ref = refs[:size], refs[size], refs[size + 1]
    for s in range(size):
        place_block(pair_ref, blocks[s], rows_at(ring_block(s, size), strip), sources)
    me = lax.axis_index("col")
    for k in range(2):
        out_ref[k] = down_dot(w_ref, pair_ref, rows_at(me ^ (1 + 2 * k), strip))


def down_far_kernel(strip, w_ref, pair_ref, out_ref):
    out_ref[...] = down_dot(w_ref, pair_ref, rows_at(lax.axis_index("col") ^ 2, strip))


def far_sum_kernel(own_ref, arrived_ref, out_ref):
    out_ref[...] = (own_ref[...] + arrived_ref[1]).astype(BF16)


def down_own_kernel(strip, w_ref, pair_ref, arrived_ref, out_ref):
    out_ref[...] = down_dot(w_ref, pair_ref, rows_at(lax.axis_index("col"), strip)) + arrived_ref[0]


def up_first_kernel(size, strip, sources, w_ref, *refs):
    blocks, pair_ref, out_ref = refs[:4], refs[4], refs[5]
    me = lax.axis_index("col")
    for s in range(4):
        place_block(pair_ref, blocks[s], rows_at(me ^ s, strip), sources)
    out_ref[...] = up_dot(w_ref, pair_ref, rows_at(ring_block(1, size), strip)).astype(BF16)


def up_rest_kernel(size, strip, w_ref, pair_ref, *out_refs):
    for s in range(2, size + 1):
        out_refs[s - 2][...] = up_dot(w_ref, pair_ref, rows_at(ring_block(s % size, size), strip))


def hop_kernel(arrived_ref, own_ref, out_ref):
    out_ref[...] = (arrived_ref[...].astype(F32) + own_ref[...]).astype(BF16)


def both_kernel(arrived_ref, own_ref, full_ref, low_ref):
    total = arrived_ref[...].astype(F32) + own_ref[...]
    full_ref[...] = total
    low_ref[...] = total.astype(BF16)


def next_up_kernel(below_ref, refl_ref, trans_ref, out_ref):
    total = below_ref[...].astype(F32) + scaled(refl_ref, trans_ref[...])
    out_ref[...] = total.astype(out_ref.dtype).reshape(out_ref.shape)


def next_down_kernel(above_ref, source_ref, refl_ref, back_ref, out_ref):
    reflected = scaled(refl_ref, back_ref[...])
    at_surface = lax.axis_index("depth") == 0

    @pl.when(at_surface)
    def _():
        out_ref[...] = (source_ref[...] + reflected).astype(out_ref.dtype).reshape(out_ref.shape)

    @pl.when(jnp.logical_not(at_surface))
    def _():
        out_ref[...] = (above_ref[...].astype(F32) + reflected).astype(out_ref.dtype).reshape(out_ref.shape)


def body(prop, source, down_init, up_init, refl_down, refl_up):
    size = lax.axis_size("row")
    assert lax.axis_size("col") == 4
    strip = down_init.shape[1]
    width = down_init.shape[2]
    sources = width // 2
    tall, wide = prop.shape[2], prop.shape[3]
    low, full = array((strip, width), BF16), array((strip, width), F32)
    factor = array((strip, LANES), F32)
    up_low, refl_below = call(ready_kernel, [low, factor], "ready_up", [up_init, refl_up])
    down_low, refl_above = call(
        ready_kernel, [low, factor], "ready_down", [down_init, refl_down], [up_low]
    )
    w = pltpu.with_memory_space_constraint(hold(prop, down_low), pltpu.VMEM)
    for sweep in range(PASSES):
        last = sweep == PASSES - 1
        near = col_swap(up_low, 1)
        far = col_swap(up_low, 2)
        if sweep == 0:
            far = behind(far, w)
        blocks_up = [up_low, near, far, col_swap(far, 1)]
        blocks_down = [down_low, ring_hop(down_low, size)]
        pair_up, travelling = call(
            functools.partial(up_first_kernel, size, strip, sources),
            [array((2, tall, width), BF16), low], "up_first", [w, *blocks_up], [blocks_down[1]],
        )
        for s in range(1, size - 1):
            blocks_down.append(ring_hop(blocks_down[-1], size))
        own_up = call(
            functools.partial(up_rest_kernel, size, strip),
            [full] * (size - 1), "up_rest", [w, pair_up], [blocks_down[1]],
        )
        pair_down, to_sibling = call(
            functools.partial(down_sibling_kernel, size, strip, sources),
            [array((2, wide, width), BF16), array((2, strip, width), F32)],
            "down_sibling", [w, *blocks_down], [own_up[0]],
        )
        from_sibling = col_swap(to_sibling, 1)
        (own_far,) = call(functools.partial(down_far_kernel, strip), [full], "down_far", [w, pair_down])
        (to_far,) = call(far_sum_kernel, [low], "far_sum", [own_far, from_sibling])
        from_far = col_swap(to_far, 2)
        (own_down,) = call(
            functools.partial(down_own_kernel, strip), [full], "down_own",             [w, pair_down, from_sibling], [to_far],
        )
        for s in range(size - 2):
            arrived = ring_hop(travelling, size)
            (travelling,) = call(
                hop_kernel, [low], "hop", [arrived, own_up[s]], [to_far] if s == size - 3 else [own_up[-1]]
            )
        back, back_low = call(
            both_kernel, [full, low], "back", [ring_hop(travelling, size), own_up[size - 2]], [own_down]
        )
        from_below = depth_shift(back_low, -1)
        trans, trans_low = call(both_kernel, [full, low], "trans", [from_far, own_down])
        from_above = depth_shift(trans_low, 1)
        kind = array((1, strip, width), F32) if last else low
        (up_low,) = call(next_up_kernel, [kind], "next_up", [from_below, refl_below, trans])
        (down_low,) = call(
            next_down_kernel, [kind], "next_down", [from_above, source, refl_above, back]
        )
    return (down_low, up_low)


def solution(mesh):
    placed = (
        P("depth", None, "row", "col"),
        P(("row", "col"), None),
        P("depth", ("row", "col"), None),
        P("depth", ("row", "col"), None),
        P("depth", ("row", "col")),
        P("depth", ("row", "col")),
    )
    return jax.shard_map(
        body,
        mesh=mesh,
        in_specs=placed,
        out_specs=(P("depth", ("row", "col"), None), P("depth", ("row", "col"), None)),
        check_vma=False,
    )
```

```python
import functools

import jax
import jax.numpy as jnp
from jax import lax
from jax.experimental import pallas as pl
from jax.experimental.pallas import tpu as pltpu
from jax.sharding import PartitionSpec as P

PASSES = 2
F32 = jnp.float32
BF16 = jnp.bfloat16
WHOLE = pl.BlockSpec(memory_space=pltpu.VMEM)
UNREAD = pl.BlockSpec(memory_space=pl.ANY)
LANES = 128
DECLARED = 21 * 10**9
CHEAP = {"up_first": 0, "split": 0}
CONTRACT_ROWS = (((0,), (0,)), ((), ()))


def ring_device(place, size):
    half = (size + 1) // 2
    if isinstance(place, int):
        return 2 * place if place < half else 2 * (size - 1 - place) + 1
    return jnp.where(place < half, 2 * place, 2 * (size - 1 - place) + 1)


def ring_place(device, size):
    return jnp.where(lax.rem(device, 2) == 0, device // 2, size - 1 - device // 2)


def ring_block(behind, size):
    place = ring_place(lax.axis_index("row"), size)
    return ring_device(lax.rem(place - behind + size, size), size)


def row_swap(x, bit):
    return lax.ppermute(x, "row", [(r, r ^ bit) for r in range(lax.axis_size("row"))])


def row_block(order, size):
    if size == 4:
        return lax.axis_index("row") ^ (0, 3, 2, 1)[order % size]
    return ring_block(order % size, size)


def ring_hop(x, size):
    pairs = [(ring_device(p, size), ring_device((p + 1) % size, size)) for p in range(size)]
    return lax.ppermute(x, "row", pairs)


def col_swap(x, bit):
    return lax.ppermute(x, "col", [(c, c ^ bit) for c in range(lax.axis_size("col"))])


def depth_shift(x, by):
    peers = lax.axis_size("depth")
    return lax.ppermute(x, "depth", [(i, i + by) for i in range(peers) if 0 <= i + by < peers])


def call(kernel, outs, name, args, after=()):
    count = len(args)

    def ordered(*refs):
        kernel(*refs[:count], *refs[count + len(after) :])

    return pl.pallas_call(
        ordered,
        in_specs=[WHOLE] * count + [UNREAD] * len(after),
        out_specs=[WHOLE] * len(outs),
        out_shape=outs,
        name=name,
        cost_estimate=pl.CostEstimate(flops=CHEAP.get(name, DECLARED), bytes_accessed=1 if name in CHEAP else 2**20, transcendentals=0),
        compiler_params=pltpu.CompilerParams(vmem_limit_bytes=12 * 2**20),
    )(*args, *after)


def array(shape, dtype):
    return jax.ShapeDtypeStruct(shape, dtype)


def behind(x, *others):
    return lax.optimization_barrier((x, *others))[0]


def rows_at(block, strip):
    return pl.ds(pl.multiple_of(block * strip, strip), strip)


def hold(prop, after):
    def kernel(w_ref, _, out_ref, sem):
        copy = pltpu.make_async_copy(w_ref, out_ref, sem)
        copy.start()
        copy.wait()

    return pl.pallas_call(
        kernel,
        in_specs=[pl.BlockSpec(memory_space=pltpu.HBM), UNREAD],
        out_specs=WHOLE,
        out_shape=pltpu.VMEM(prop.shape, prop.dtype),
        scratch_shapes=[pltpu.SemaphoreType.DMA],
        name="hold",
        cost_estimate=pl.CostEstimate(flops=0, bytes_accessed=40 * prop.size, transcendentals=0),
        compiler_params=pltpu.CompilerParams(vmem_limit_bytes=36 * 2**20),
    )(prop, after)


def place_block(pair_ref, block_ref, rows, sources):
    values = block_ref[...]
    pair_ref[0, rows, :] = values
    pair_ref[1, rows, :sources] = -values[:, sources:]
    pair_ref[1, rows, sources:] = values[:, :sources]


def spread(refl_ref):
    return jnp.broadcast_to(refl_ref[...], (LANES, refl_ref.shape[1])).T


def scaled(refl_ref, values):
    factor = refl_ref[...]
    pieces = [factor * values[:, k : k + LANES] for k in range(0, values.shape[1], LANES)]
    return jnp.concatenate(pieces, axis=1)


def ready_kernel(field_ref, refl_ref, low_ref, factor_ref):
    low_ref[...] = field_ref[0].astype(BF16)
    factor_ref[...] = spread(refl_ref)


def down_dot(w_ref, pair_ref, rows):
    return jnp.dot(w_ref[0, 0, rows, :], pair_ref[0], preferred_element_type=F32) + jnp.dot(
        w_ref[0, 1, rows, :], pair_ref[1], preferred_element_type=F32
    )


def split_kernel(whole_ref, *part_refs):
    half = whole_ref.shape[0] // 2
    for k, ref in enumerate(part_refs):
        ref[...] = whole_ref[k * half : (k + 1) * half, :]


def up_dot(w_ref, pair_ref, columns):
    return lax.dot_general(
        w_ref[0, 0, :, columns], pair_ref[0], CONTRACT_ROWS, preferred_element_type=F32
    ) + lax.dot_general(w_ref[0, 1, :, columns], pair_ref[1], CONTRACT_ROWS, preferred_element_type=F32)


def down_sibling_kernel(size, strip, sources, w_ref, *refs):
    blocks, pair_ref, out_ref = refs[:size], refs[size], refs[size + 1]
    for s in range(size):
        place_block(pair_ref, blocks[s], rows_at(row_block(s, size), strip), sources)
    me = lax.axis_index("col")
    for k in range(2):
        out_ref[k] = down_dot(w_ref, pair_ref, rows_at(me ^ (1 + 2 * k), strip))


def down_far_kernel(strip, w_ref, pair_ref, out_ref):
    out_ref[...] = down_dot(w_ref, pair_ref, rows_at(lax.axis_index("col") ^ 2, strip))


def far_sum_kernel(own_ref, arrived_ref, out_ref):
    out_ref[...] = (own_ref[...] + arrived_ref[1]).astype(BF16)


def down_own_kernel(strip, w_ref, pair_ref, arrived_ref, out_ref):
    out_ref[...] = down_dot(w_ref, pair_ref, rows_at(lax.axis_index("col"), strip)) + arrived_ref[0]


def up_first_kernel(size, strip, sources, w_ref, *refs):
    *blocks, pair_ref, out_ref = refs
    me = lax.axis_index("col")
    for s in range(2):
        place_block(pair_ref, blocks[s], rows_at(me ^ s, strip), sources)
    for s in range(4):
        part = rows_at(2 * (me ^ (2 + s // 2)) + s % 2, strip // 2)
        place_block(pair_ref, blocks[2 + s], part, sources)
    out_ref[...] = up_dot(w_ref, pair_ref, rows_at(row_block(1, size), strip)).astype(BF16)


def up_rest_kernel(size, strip, w_ref, pair_ref, *out_refs):
    for s, ref in zip(range(2, size + 1), out_refs):
        ref[...] = up_dot(w_ref, pair_ref, rows_at(row_block(s, size), strip)).astype(ref.dtype)


def hop_kernel(arrived_ref, own_ref, out_ref):
    out_ref[...] = (arrived_ref[...].astype(F32) + own_ref[...]).astype(BF16)


def both_kernel(*refs):
    *arrived, own_ref, full_ref, low_ref = refs
    total = own_ref[...]
    for ref in arrived:
        total = total + ref[...].astype(F32)
    full_ref[...] = total
    low_ref[...] = total.astype(BF16)


def sums_kernel(count, *refs):
    back_full, trans_full, low_ref = refs[-3:]
    own_up, from_far, own_down = refs[count : count + 3]
    back = own_up[...]
    for ref in refs[:count]:
        back = back + ref[...].astype(F32)
    trans = own_down[...] + from_far[...].astype(F32)
    back_full[...] = back
    trans_full[...] = trans
    at_surface = lax.axis_index("depth") == 0

    @pl.when(at_surface)
    def _():
        low_ref[...] = trans.astype(BF16)

    @pl.when(jnp.logical_not(at_surface))
    def _():
        low_ref[...] = back.astype(BF16)


def next_kernel(above_ref, below_ref, source_ref, factor_down, factor_up, back_ref, trans_ref, down_ref, up_ref):
    place, last = lax.axis_index("depth"), lax.axis_size("depth") - 1
    down = scaled(factor_down, back_ref[...])
    up = scaled(factor_up, trans_ref[...])

    def put(ref, value):
        ref[...] = value.astype(ref.dtype).reshape(ref.shape)

    @pl.when(place == 0)
    def _():
        put(down_ref, source_ref[...] + down)

    @pl.when(place > 0)
    def _():
        put(down_ref, above_ref[...].astype(F32) + down)

    @pl.when(place == last)
    def _():
        put(up_ref, up)

    @pl.when(place < last)
    def _():
        put(up_ref, below_ref[...].astype(F32) + up)


def body(prop, source, down_init, up_init, refl_down, refl_up):
    size = lax.axis_size("row")
    assert lax.axis_size("col") == 4
    strip = down_init.shape[1]
    width = down_init.shape[2]
    sources = width // 2
    tall, wide = prop.shape[2], prop.shape[3]
    low, full = array((strip, width), BF16), array((strip, width), F32)
    factor = array((strip, LANES), F32)
    up_low, refl_below = call(ready_kernel, [low, factor], "ready_up", [up_init, refl_up])
    down_low, refl_above = call(
        ready_kernel, [low, factor], "ready_down", [down_init, refl_down], [up_low]
    )
    w = pltpu.with_memory_space_constraint(hold(prop, down_low), pltpu.VMEM)
    for sweep in range(PASSES):
        last = sweep == PASSES - 1
        near = col_swap(up_low, 1)
        far = col_swap(up_low, 2)
        if sweep == 0:
            far = behind(far, w)
        parts = call(split_kernel, [array((strip // 2, width), BF16)] * 2, "split", [far])
        blocks_up = [up_low, near, *parts, col_swap(parts[0], 1), col_swap(parts[1], 1)]
        if size == 4:
            beside, across = row_swap(down_low, 1), row_swap(down_low, 2)
            begun, ready = [], [across, beside]
        else:
            blocks_down = [down_low]
            for s in range(size - 1):
                blocks_down.append(ring_hop(blocks_down[-1], size))
            begun = ready = blocks_down[1:2]
        pair_up, travelling = call(
            functools.partial(up_first_kernel, size, strip, sources),
            [array((2, tall, width), BF16), low], "up_first", [w, *blocks_up], begun,
        )
        if size == 4:
            blocks_down = [down_low, row_swap(behind(across, travelling), 1), across, beside]
        kinds = [full, low, full] if size == 4 else [full] * (size - 1)
        own_up = call(
            functools.partial(up_rest_kernel, size, strip), kinds, "up_rest", [w, pair_up], ready,
        )
        if size == 4:
            (passed,) = call(
                hop_kernel, [low], "hop", [row_swap(travelling, 1), own_up[0]], [own_up[1]]
            )
            arrived = [row_swap(behind(own_up[1], passed), 1), row_swap(passed, 2)]
            before_down = [passed]
        else:
            for s in range(size - 2):
                (travelling,) = call(
                    hop_kernel, [low], "hop", [ring_hop(travelling, size), own_up[s]], [own_up[-1]]
                )
            arrived = [ring_hop(travelling, size)]
            before_down = [own_up[0]]
        pair_down, to_sibling = call(
            functools.partial(down_sibling_kernel, size, strip, sources),
            [array((2, wide, width), BF16), array((2, strip, width), F32)],
            "down_sibling", [w, *blocks_down], before_down,
        )
        from_sibling = col_swap(to_sibling, 1)
        (own_far,) = call(functools.partial(down_far_kernel, strip), [full], "down_far", [w, pair_down])
        (to_far,) = call(far_sum_kernel, [low], "far_sum", [own_far, from_sibling])
        from_far = col_swap(to_far, 2)
        (own_down,) = call(
            functools.partial(down_own_kernel, strip), [full], "down_own",
            [w, pair_down, from_sibling], [to_far],
        )
        if lax.axis_size("depth") == 2:
            back, trans, passed_on = call(
                functools.partial(sums_kernel, len(arrived)), [full, full, low], "sums",
                [*arrived, own_up[-1], from_far, own_down],
            )
            from_above = from_below = lax.ppermute(passed_on, "depth", [(0, 1), (1, 0)])
        else:
            back, back_low = call(both_kernel, [full, low], "back", [*arrived, own_up[-1]], [own_down])
            from_below = depth_shift(back_low, -1)
            trans, trans_low = call(both_kernel, [full, low], "trans", [from_far, own_down])
            from_above = depth_shift(trans_low, 1)
        kind = array((1, strip, width), F32) if last else low
        down_low, up_low = call(
            next_kernel, [kind, kind], "next",
            [from_above, from_below, source, refl_above, refl_below, back, trans],
        )
    return (down_low, up_low)


def solution(mesh):
    placed = (
        P("depth", None, "row", "col"),
        P(("row", "col"), None),
        P("depth", ("row", "col"), None),
        P("depth", ("row", "col"), None),
        P("depth", ("row", "col")),
        P("depth", ("row", "col")),
    )
    return jax.shard_map(
        body,
        mesh=mesh,
        in_specs=placed,
        out_specs=(P("depth", ("row", "col"), None), P("depth", ("row", "col"), None)),
        check_vma=False,
    )
```

```python
import functools

import jax
import jax.numpy as jnp
from jax import lax
from jax.experimental import pallas as pl
from jax.experimental.pallas import tpu as pltpu
from jax.sharding import PartitionSpec as P

PASSES = 2
F32 = jnp.float32
BF16 = jnp.bfloat16
WHOLE = pl.BlockSpec(memory_space=pltpu.VMEM)
UNREAD = pl.BlockSpec(memory_space=pl.ANY)
LANES = 128
DECLARED = 21 * 10**9
CHEAP = {"up_first": 0, "split": 0, "down_own": 0}
CONTRACT_ROWS = (((0,), (0,)), ((), ()))


def ring_device(place, size):
    half = (size + 1) // 2
    if isinstance(place, int):
        return 2 * place if place < half else 2 * (size - 1 - place) + 1
    return jnp.where(place < half, 2 * place, 2 * (size - 1 - place) + 1)


def ring_place(device, size):
    return jnp.where(lax.rem(device, 2) == 0, device // 2, size - 1 - device // 2)


def ring_block(behind, size):
    place = ring_place(lax.axis_index("row"), size)
    return ring_device(lax.rem(place - behind + size, size), size)


def row_swap(x, bit):
    return lax.ppermute(x, "row", [(r, r ^ bit) for r in range(lax.axis_size("row"))])


def row_block(order, size):
    if size == 4:
        return lax.axis_index("row") ^ (0, 3, 2, 1)[order % size]
    return ring_block(order % size, size)


def ring_hop(x, size):
    pairs = [(ring_device(p, size), ring_device((p + 1) % size, size)) for p in range(size)]
    return lax.ppermute(x, "row", pairs)


def col_swap(x, bit):
    return lax.ppermute(x, "col", [(c, c ^ bit) for c in range(lax.axis_size("col"))])


def depth_shift(x, by):
    peers = lax.axis_size("depth")
    return lax.ppermute(x, "depth", [(i, i + by) for i in range(peers) if 0 <= i + by < peers])


def call(kernel, outs, name, args, after=()):
    count = len(args)

    def ordered(*refs):
        kernel(*refs[:count], *refs[count + len(after) :])

    return pl.pallas_call(
        ordered,
        in_specs=[WHOLE] * count + [UNREAD] * len(after),
        out_specs=[WHOLE] * len(outs),
        out_shape=outs,
        name=name,
        cost_estimate=pl.CostEstimate(flops=CHEAP.get(name, DECLARED), bytes_accessed=1 if name in CHEAP else 2**20, transcendentals=0),
        compiler_params=pltpu.CompilerParams(vmem_limit_bytes=12 * 2**20),
    )(*args, *after)


def array(shape, dtype):
    return jax.ShapeDtypeStruct(shape, dtype)


def behind(x, *others):
    return lax.optimization_barrier((x, *others))[0]


def rows_at(block, strip):
    return pl.ds(pl.multiple_of(block * strip, strip), strip)


def place_block(pair_ref, block_ref, rows, sources):
    values = block_ref[...]
    pair_ref[0, rows, :] = values
    pair_ref[1, rows, :sources] = -values[:, sources:]
    pair_ref[1, rows, sources:] = values[:, :sources]


def spread(refl_ref):
    return jnp.broadcast_to(refl_ref[...], (LANES, refl_ref.shape[1])).T


def scaled(refl_ref, values):
    factor = refl_ref[...]
    pieces = [factor * values[:, k : k + LANES] for k in range(0, values.shape[1], LANES)]
    return jnp.concatenate(pieces, axis=1)


def ready_kernel(field_ref, low_ref):
    low_ref[...] = field_ref[0].astype(BF16)


def factor_kernel(down_ref, up_ref, down_factor, up_factor):
    down_factor[...] = spread(down_ref)
    up_factor[...] = spread(up_ref)


def down_dot(w_ref, pair_ref, rows):
    return jnp.dot(w_ref[0, 0, rows, :], pair_ref[0], preferred_element_type=F32) + jnp.dot(
        w_ref[0, 1, rows, :], pair_ref[1], preferred_element_type=F32
    )


def split_kernel(whole_ref, *part_refs):
    half = whole_ref.shape[0] // 2
    for k, ref in enumerate(part_refs):
        ref[...] = whole_ref[k * half : (k + 1) * half, :]


def up_dot(w_ref, pair_ref, columns):
    return lax.dot_general(
        w_ref[0, 0, :, columns], pair_ref[0], CONTRACT_ROWS, preferred_element_type=F32
    ) + lax.dot_general(w_ref[0, 1, :, columns], pair_ref[1], CONTRACT_ROWS, preferred_element_type=F32)


def down_sibling_kernel(size, strip, sources, w_ref, *refs):
    blocks, pair_ref, out_ref = refs[:size], refs[size], refs[size + 1]
    for s in range(size):
        place_block(pair_ref, blocks[s], rows_at(row_block(s, size), strip), sources)
    out_ref[...] = down_dot(w_ref, pair_ref, rows_at(lax.axis_index("col") ^ 3, strip))


def down_kernel(strip, apart, w_ref, pair_ref, out_ref):
    out_ref[...] = down_dot(w_ref, pair_ref, rows_at(lax.axis_index("col") ^ apart, strip))


def far_sum_kernel(own_ref, arrived_ref, out_ref):
    out_ref[...] = (own_ref[...] + arrived_ref[...]).astype(BF16)


def down_near_kernel(strip, w_ref, pair_ref, *part_refs):
    half = strip // 2
    for k, ref in enumerate(part_refs):
        rows = rows_at(2 * (lax.axis_index("col") ^ 1) + k, half)
        ref[...] = down_dot(w_ref, pair_ref, rows).astype(BF16)


def down_own_kernel(strip, w_ref, pair_ref, first_ref, second_ref, out_ref):
    half = strip // 2
    for k, ref in enumerate((first_ref, second_ref)):
        rows = rows_at(2 * lax.axis_index("col") + k, half)
        out_ref[k * half : (k + 1) * half, :] = down_dot(w_ref, pair_ref, rows) + ref[...].astype(F32)


def up_first_kernel(size, strip, sources, w_ref, *refs):
    *blocks, pair_ref, out_ref = refs
    me = lax.axis_index("col")
    for s in range(2):
        place_block(pair_ref, blocks[s], rows_at(me ^ s, strip), sources)
    for s in range(4):
        part = rows_at(2 * (me ^ (2 + s // 2)) + s % 2, strip // 2)
        place_block(pair_ref, blocks[2 + s], part, sources)
    out_ref[...] = up_dot(w_ref, pair_ref, rows_at(row_block(1, size), strip)).astype(BF16)


def up_rest_kernel(size, strip, w_ref, pair_ref, *out_refs):
    for s, ref in zip(range(2, size + 1), out_refs):
        ref[...] = up_dot(w_ref, pair_ref, rows_at(row_block(s, size), strip)).astype(ref.dtype)


def hop_kernel(arrived_ref, own_ref, out_ref):
    out_ref[...] = (arrived_ref[...].astype(F32) + own_ref[...]).astype(BF16)


def both_kernel(*refs):
    *arrived, own_ref, full_ref, low_ref = refs
    total = own_ref[...]
    for ref in arrived:
        total = total + ref[...].astype(F32)
    full_ref[...] = total
    low_ref[...] = total.astype(BF16)


def sums_kernel(count, *refs):
    back_full, trans_full, low_ref = refs[-3:]
    own_up, from_far, own_down = refs[count : count + 3]
    back = own_up[...]
    for ref in refs[:count]:
        back = back + ref[...].astype(F32)
    trans = own_down[...] + from_far[...].astype(F32)
    back_full[...] = back
    trans_full[...] = trans
    at_surface = lax.axis_index("depth") == 0

    @pl.when(at_surface)
    def _():
        low_ref[...] = trans.astype(BF16)

    @pl.when(jnp.logical_not(at_surface))
    def _():
        low_ref[...] = back.astype(BF16)


def next_kernel(above_ref, below_ref, source_ref, factor_down, factor_up, back_ref, trans_ref, down_ref, up_ref):
    place, last = lax.axis_index("depth"), lax.axis_size("depth") - 1
    down = scaled(factor_down, back_ref[...])
    up = scaled(factor_up, trans_ref[...])

    def put(ref, value):
        ref[...] = value.astype(ref.dtype).reshape(ref.shape)

    @pl.when(place == 0)
    def _():
        put(down_ref, source_ref[...] + down)

    @pl.when(place > 0)
    def _():
        put(down_ref, above_ref[...].astype(F32) + down)

    @pl.when(place == last)
    def _():
        put(up_ref, up)

    @pl.when(place < last)
    def _():
        put(up_ref, below_ref[...].astype(F32) + up)


def body(prop, source, down_init, up_init, refl_down, refl_up):
    size = lax.axis_size("row")
    assert lax.axis_size("col") == 4
    strip = down_init.shape[1]
    width = down_init.shape[2]
    sources = width // 2
    tall, wide = prop.shape[2], prop.shape[3]
    low, full = array((strip, width), BF16), array((strip, width), F32)
    factor = array((strip, LANES), F32)
    (up_low,) = call(ready_kernel, [low], "ready_up", [up_init])
    (down_low,) = call(ready_kernel, [low], "ready_down", [down_init], [up_low])
    w = prop
    for sweep in range(PASSES):
        last = sweep == PASSES - 1
        near = col_swap(up_low, 1)
        far = col_swap(up_low, 2)
        if sweep == 0:
            far = behind(far, down_low)
        parts = call(split_kernel, [array((strip // 2, width), BF16)] * 2, "split", [far])
        blocks_up = [up_low, near, *parts, col_swap(parts[0], 1), col_swap(parts[1], 1)]
        if size == 4:
            beside, across = row_swap(down_low, 1), row_swap(down_low, 2)
            begun, ready = [], [across, beside]
        else:
            blocks_down = [down_low]
            for s in range(size - 1):
                blocks_down.append(ring_hop(blocks_down[-1], size))
            begun = ready = blocks_down[1:2]
        pair_up, travelling = call(
            functools.partial(up_first_kernel, size, strip, sources),
            [array((2, tall, width), BF16), low], "up_first", [w, *blocks_up], begun,
        )
        if size == 4:
            blocks_down = [down_low, row_swap(behind(across, travelling), 1), across, beside]
        kinds = [full, low, full] if size == 4 else [full] * (size - 1)
        own_up = call(
            functools.partial(up_rest_kernel, size, strip), kinds, "up_rest", [w, pair_up], ready,
        )
        if size == 4:
            (passed,) = call(
                hop_kernel, [low], "hop", [row_swap(travelling, 1), own_up[0]], [own_up[1]]
            )
            arrived = [row_swap(behind(own_up[1], passed), 1), row_swap(passed, 2)]
            before_down = [passed]
        else:
            for s in range(size - 2):
                (travelling,) = call(
                    hop_kernel, [low], "hop", [ring_hop(travelling, size), own_up[s]], [own_up[-1]]
                )
            arrived = [ring_hop(travelling, size)]
            before_down = [own_up[0]]
        pair_down, to_sibling = call(
            functools.partial(down_sibling_kernel, size, strip, sources),
            [array((2, wide, width), BF16), full],
            "down_sibling", [w, *blocks_down], before_down,
        )
        (own_far,) = call(functools.partial(down_kernel, strip, 2), [full], "down_far", [w, pair_down])
        (to_far,) = call(far_sum_kernel, [low], "far_sum", [own_far, col_swap(to_sibling, 1)])
        from_far = col_swap(to_far, 2)
        parts = call(
            functools.partial(down_near_kernel, strip), [array((strip // 2, width), BF16)] * 2,
            "down_near", [w, pair_down], [to_far],
        )
        (own_down,) = call(
            functools.partial(down_own_kernel, strip), [full], "down_own",
            [w, pair_down, *(col_swap(part, 1) for part in parts)],
        )
        if sweep == 0:
            refl_above, refl_below = call(
                factor_kernel, [factor] * 2, "factors", [refl_down, refl_up], [own_down]
            )
        if lax.axis_size("depth") == 2:
            back, trans, passed_on = call(
                functools.partial(sums_kernel, len(arrived)), [full, full, low], "sums",
                [*arrived, own_up[-1], from_far, own_down],
            )
            from_above = from_below = lax.ppermute(passed_on, "depth", [(0, 1), (1, 0)])
        else:
            back, back_low = call(both_kernel, [full, low], "back", [*arrived, own_up[-1]], [own_down])
            from_below = depth_shift(back_low, -1)
            trans, trans_low = call(both_kernel, [full, low], "trans", [from_far, own_down])
            from_above = depth_shift(trans_low, 1)
        kind = array((1, strip, width), F32) if last else low
        down_low, up_low = call(
            next_kernel, [kind, kind], "next",
            [from_above, from_below, source, refl_above, refl_below, back, trans],
        )
    return (down_low, up_low)


def solution(mesh):
    placed = (
        P("depth", None, "row", "col"),
        P(("row", "col"), None),
        P("depth", ("row", "col"), None),
        P("depth", ("row", "col"), None),
        P("depth", ("row", "col")),
        P("depth", ("row", "col")),
    )
    return jax.shard_map(
        body,
        mesh=mesh,
        in_specs=placed,
        out_specs=(P("depth", ("row", "col"), None), P("depth", ("row", "col"), None)),
        check_vma=False,
    )
```

```python
import functools

import jax
import jax.numpy as jnp
from jax import lax
from jax.experimental import pallas as pl
from jax.experimental.pallas import tpu as pltpu
from jax.sharding import PartitionSpec as P

PASSES = 2
F32 = jnp.float32
BF16 = jnp.bfloat16
WHOLE = pl.BlockSpec(memory_space=pltpu.VMEM)
UNREAD = pl.BlockSpec(memory_space=pl.ANY)
LANES = 128
DECLARED = 21 * 10**9
CHEAP = {"up_first": 0, "split": 0, "down_own": 0}
CONTRACT_ROWS = (((0,), (0,)), ((), ()))


def ring_device(place, size):
    half = (size + 1) // 2
    if isinstance(place, int):
        return 2 * place if place < half else 2 * (size - 1 - place) + 1
    return jnp.where(place < half, 2 * place, 2 * (size - 1 - place) + 1)


def ring_place(device, size):
    return jnp.where(lax.rem(device, 2) == 0, device // 2, size - 1 - device // 2)


def ring_block(behind, size):
    place = ring_place(lax.axis_index("row"), size)
    return ring_device(lax.rem(place - behind + size, size), size)


def row_swap(x, bit):
    return lax.ppermute(x, "row", [(r, r ^ bit) for r in range(lax.axis_size("row"))])


def row_block(order, size):
    if size == 4:
        return lax.axis_index("row") ^ (0, 3, 2, 1)[order % size]
    return ring_block(order % size, size)


def ring_hop(x, size):
    pairs = [(ring_device(p, size), ring_device((p + 1) % size, size)) for p in range(size)]
    return lax.ppermute(x, "row", pairs)


def col_swap(x, bit):
    return lax.ppermute(x, "col", [(c, c ^ bit) for c in range(lax.axis_size("col"))])


def depth_shift(x, by):
    peers = lax.axis_size("depth")
    return lax.ppermute(x, "depth", [(i, i + by) for i in range(peers) if 0 <= i + by < peers])


def call(kernel, outs, name, args, after=()):
    count = len(args)

    def ordered(*refs):
        kernel(*refs[:count], *refs[count + len(after) :])

    return pl.pallas_call(
        ordered,
        in_specs=[WHOLE] * count + [UNREAD] * len(after),
        out_specs=[WHOLE] * len(outs),
        out_shape=outs,
        name=name,
        cost_estimate=pl.CostEstimate(flops=CHEAP.get(name, DECLARED), bytes_accessed=1 if name in CHEAP else 2**20, transcendentals=0),
        compiler_params=pltpu.CompilerParams(vmem_limit_bytes=12 * 2**20),
    )(*args, *after)


def array(shape, dtype):
    return jax.ShapeDtypeStruct(shape, dtype)


def behind(x, *others):
    return lax.optimization_barrier((x, *others))[0]


def rows_at(block, strip):
    return pl.ds(pl.multiple_of(block * strip, strip), strip)


def place_block(pair_ref, block_ref, rows, sources):
    values = block_ref[...]
    pair_ref[0, rows, :] = values
    pair_ref[1, rows, :sources] = -values[:, sources:]
    pair_ref[1, rows, sources:] = values[:, :sources]


def spread(refl_ref):
    return jnp.broadcast_to(refl_ref[...], (LANES, refl_ref.shape[1])).T


def scaled(refl_ref, values):
    factor = refl_ref[...]
    pieces = [factor * values[:, k : k + LANES] for k in range(0, values.shape[1], LANES)]
    return jnp.concatenate(pieces, axis=1)


def ready_kernel(field_ref, low_ref):
    low_ref[...] = field_ref[0].astype(BF16)


def factor_kernel(down_ref, up_ref, down_factor, up_factor):
    down_factor[...] = spread(down_ref)
    up_factor[...] = spread(up_ref)


def down_dot(w_ref, pair_ref, rows):
    return jnp.dot(w_ref[0, 0, rows, :], pair_ref[0], preferred_element_type=F32) + jnp.dot(
        w_ref[0, 1, rows, :], pair_ref[1], preferred_element_type=F32
    )


def split_kernel(whole_ref, *part_refs):
    half = whole_ref.shape[0] // 2
    for k, ref in enumerate(part_refs):
        ref[...] = whole_ref[k * half : (k + 1) * half, :]


def up_dot(w_ref, pair_ref, columns):
    return lax.dot_general(
        w_ref[0, 0, :, columns], pair_ref[0], CONTRACT_ROWS, preferred_element_type=F32
    ) + lax.dot_general(w_ref[0, 1, :, columns], pair_ref[1], CONTRACT_ROWS, preferred_element_type=F32)


def down_sibling_kernel(size, strip, sources, w_ref, *refs):
    blocks, pair_ref, out_ref = refs[:size], refs[size], refs[size + 1]
    for s in range(size):
        place_block(pair_ref, blocks[s], rows_at(row_block(s, size), strip), sources)
    out_ref[...] = down_dot(w_ref, pair_ref, rows_at(lax.axis_index("col") ^ 3, strip))


def down_kernel(strip, apart, w_ref, pair_ref, out_ref):
    out_ref[...] = down_dot(w_ref, pair_ref, rows_at(lax.axis_index("col") ^ apart, strip))


def far_sum_kernel(own_ref, arrived_ref, out_ref):
    out_ref[...] = (own_ref[...] + arrived_ref[...]).astype(BF16)


def down_near_kernel(strip, w_ref, pair_ref, *part_refs):
    half = strip // 2
    for k, ref in enumerate(part_refs):
        rows = rows_at(2 * (lax.axis_index("col") ^ 1) + k, half)
        ref[...] = down_dot(w_ref, pair_ref, rows).astype(BF16)


def down_own_kernel(strip, w_ref, pair_ref, first_ref, second_ref, out_ref):
    half = strip // 2
    for k, ref in enumerate((first_ref, second_ref)):
        rows = rows_at(2 * lax.axis_index("col") + k, half)
        out_ref[k * half : (k + 1) * half, :] = down_dot(w_ref, pair_ref, rows) + ref[...].astype(F32)


def up_first_kernel(size, strip, sources, w_ref, *refs):
    *blocks, pair_ref, out_ref = refs
    me = lax.axis_index("col")
    for s in range(2):
        place_block(pair_ref, blocks[s], rows_at(me ^ s, strip), sources)
    for s in range(4):
        part = rows_at(2 * (me ^ (2 + s // 2)) + s % 2, strip // 2)
        place_block(pair_ref, blocks[2 + s], part, sources)
    out_ref[...] = up_dot(w_ref, pair_ref, rows_at(row_block(1, size), strip)).astype(BF16)


def up_rest_kernel(size, strip, first, w_ref, pair_ref, *out_refs):
    for s, ref in zip(range(first, size + 1), out_refs):
        ref[...] = up_dot(w_ref, pair_ref, rows_at(row_block(s, size), strip)).astype(ref.dtype)


def hop_kernel(arrived_ref, own_ref, out_ref):
    out_ref[...] = (arrived_ref[...].astype(F32) + own_ref[...]).astype(BF16)


def both_kernel(*refs):
    *arrived, own_ref, full_ref, low_ref = refs
    total = own_ref[...]
    for ref in arrived:
        total = total + ref[...].astype(F32)
    full_ref[...] = total
    low_ref[...] = total.astype(BF16)


def sums_kernel(count, *refs):
    back_full, trans_full, low_ref = refs[-3:]
    own_up, from_far, own_down = refs[count : count + 3]
    back = own_up[...]
    for ref in refs[:count]:
        back = back + ref[...].astype(F32)
    trans = own_down[...] + from_far[...].astype(F32)
    back_full[...] = back
    trans_full[...] = trans
    at_surface = lax.axis_index("depth") == 0

    @pl.when(at_surface)
    def _():
        low_ref[...] = trans.astype(BF16)

    @pl.when(jnp.logical_not(at_surface))
    def _():
        low_ref[...] = back.astype(BF16)


def next_kernel(above_ref, below_ref, source_ref, factor_down, factor_up, back_ref, trans_ref, down_ref, up_ref):
    place, last = lax.axis_index("depth"), lax.axis_size("depth") - 1
    down = scaled(factor_down, back_ref[...])
    up = scaled(factor_up, trans_ref[...])

    def put(ref, value):
        ref[...] = value.astype(ref.dtype).reshape(ref.shape)

    @pl.when(place == 0)
    def _():
        put(down_ref, source_ref[...] + down)

    @pl.when(place > 0)
    def _():
        put(down_ref, above_ref[...].astype(F32) + down)

    @pl.when(place == last)
    def _():
        put(up_ref, up)

    @pl.when(place < last)
    def _():
        put(up_ref, below_ref[...].astype(F32) + up)


def body(prop, source, down_init, up_init, refl_down, refl_up):
    size = lax.axis_size("row")
    assert lax.axis_size("col") == 4
    strip = down_init.shape[1]
    width = down_init.shape[2]
    sources = width // 2
    tall, wide = prop.shape[2], prop.shape[3]
    low, full = array((strip, width), BF16), array((strip, width), F32)
    factor = array((strip, LANES), F32)
    (up_low,) = call(ready_kernel, [low], "ready_up", [up_init])
    (down_low,) = call(ready_kernel, [low], "ready_down", [down_init], [up_low])
    w = prop
    for sweep in range(PASSES):
        last = sweep == PASSES - 1
        near = col_swap(up_low, 1)
        far = col_swap(up_low, 2)
        if sweep == 0:
            far = behind(far, down_low)
        parts = call(split_kernel, [array((strip // 2, width), BF16)] * 2, "split", [far])
        blocks_up = [up_low, near, *parts, col_swap(parts[0], 1), col_swap(parts[1], 1)]
        if size == 4:
            beside, across = row_swap(down_low, 1), row_swap(down_low, 2)
            begun, ready = [], [across, beside]
        else:
            blocks_down = [down_low]
            for s in range(size - 1):
                blocks_down.append(ring_hop(blocks_down[-1], size))
            begun = ready = blocks_down[1:2]
        pair_up, travelling = call(
            functools.partial(up_first_kernel, size, strip, sources),
            [array((2, tall, width), BF16), low], "up_first", [w, *blocks_up], begun,
        )
        if size == 4:
            blocks_down = [down_low, row_swap(behind(across, travelling), 1), across, beside]
        kinds = [full, low, full] if size == 4 else [full] * (size - 1)
        own_up = call(
            functools.partial(up_rest_kernel, size, strip, 2), kinds[:1] if size == 4 else kinds, "up_second", [w, pair_up], ready,
        )
        if size == 4:
            (passed,) = call(hop_kernel, [low], "hop", [row_swap(travelling, 1), own_up[0]])
            own_up += call(
                functools.partial(up_rest_kernel, size, strip, 3), kinds[1:], "up_rest", [w, pair_up], [passed]
            )
            arrived = [row_swap(behind(own_up[1], passed), 1), row_swap(passed, 2)]
            before_down = [passed]
        else:
            for s in range(size - 2):
                (travelling,) = call(
                    hop_kernel, [low], "hop", [ring_hop(travelling, size), own_up[s]], [own_up[-1]]
                )
            arrived = [ring_hop(travelling, size)]
            before_down = [own_up[0]]
        pair_down, to_sibling = call(
            functools.partial(down_sibling_kernel, size, strip, sources),
            [array((2, wide, width), BF16), full],
            "down_sibling", [w, *blocks_down], before_down,
        )
        (own_far,) = call(functools.partial(down_kernel, strip, 2), [full], "down_far", [w, pair_down])
        (to_far,) = call(far_sum_kernel, [low], "far_sum", [own_far, col_swap(to_sibling, 1)])
        from_far = col_swap(to_far, 2)
        parts = call(
            functools.partial(down_near_kernel, strip), [array((strip // 2, width), BF16)] * 2,
            "down_near", [w, pair_down], [to_far],
        )
        (own_down,) = call(
            functools.partial(down_own_kernel, strip), [full], "down_own",
            [w, pair_down, *(col_swap(part, 1) for part in parts)],
        )
        if sweep == 0:
            refl_above, refl_below = call(
                factor_kernel, [factor] * 2, "factors", [refl_down, refl_up], [own_down]
            )
        if lax.axis_size("depth") == 2:
            back, trans, passed_on = call(
                functools.partial(sums_kernel, len(arrived)), [full, full, low], "sums",
                [*arrived, own_up[-1], from_far, own_down],
            )
            from_above = from_below = lax.ppermute(passed_on, "depth", [(0, 1), (1, 0)])
        else:
            back, back_low = call(both_kernel, [full, low], "back", [*arrived, own_up[-1]], [own_down])
            from_below = depth_shift(back_low, -1)
            trans, trans_low = call(both_kernel, [full, low], "trans", [from_far, own_down])
            from_above = depth_shift(trans_low, 1)
        kind = array((1, strip, width), F32) if last else low
        down_low, up_low = call(
            next_kernel, [kind, kind], "next",
            [from_above, from_below, source, refl_above, refl_below, back, trans],
        )
    return (down_low, up_low)


def solution(mesh):
    placed = (
        P("depth", None, "row", "col"),
        P(("row", "col"), None),
        P("depth", ("row", "col"), None),
        P("depth", ("row", "col"), None),
        P("depth", ("row", "col")),
        P("depth", ("row", "col")),
    )
    return jax.shard_map(
        body,
        mesh=mesh,
        in_specs=placed,
        out_specs=(P("depth", ("row", "col"), None), P("depth", ("row", "col"), None)),
        check_vma=False,
    )
```
